32 devices in a mesh: gx: 4 (over x, core), gy: 2 (over y), gz: 4 (over z).
Axes of the slice: x: 2, y: 2, z: 4, core: 2. Of those that a mesh axis runs over, the one named last changes fastest.
Arguments:
- hidden_in: bfloat16 [32, 16384], P(('gy', 'gz'), 'gx'), may hold values from -4 to 4
- segments: int32 [32], replicated, may hold values from 0 to 3, never falling along the last dimension, each value on 1 to 16 neighbouring positions
- attn_gain: float32 [16384], P('gx'), may hold values from 0.1 to 1.9
- query_weight: bfloat16 [16384, 16384], P('gx', ('gy', 'gz')), may hold values from -32 to 32
- key_weight: bfloat16 [16384, 1024], P('gx', 'gy'), may hold values from -0.046875 to 0.046875
- value_weight: bfloat16 [16384, 1024], P('gx', 'gy'), may hold values from -0.046875 to 0.046875
- output_weight: bfloat16 [16384, 16384], P(('gy', 'gz'), 'gx'), may hold values from -0.1875 to 0.1875
- ffn_gain: float32 [16384], P('gx'), may hold values from 0.1 to 1.9
- gate_weight: bfloat16 [16384, 32768], P('gx', ('gy', 'gz')), may hold values from -0.046875 to 0.046875
Outputs:
- datastore_keys: bfloat16 [32, 32768], P('gx', ('gy', 'gz'))
The draws below stay inside these ranges and needn't reach their ends.
All inputs are finite; a program needn't handle non-finite values.
Results may differ from the reference program's by a relative error of at most 0.0085.
Values may be sent and summed in bfloat16 or wider, within the bound.
A program may use at most 128 MiB of HBM per device.

```python
import math
import jax
import jax.numpy as jnp
import numpy as np
from jax import lax

D = 16384
QH = 128
KVH = 8
HS = 128
G = 32768
TOKENS = 32


def draw_query_weight(key, part):
    values = jax.random.truncated_normal(key, -6.0, 6.0, (D, QH * HS), jnp.float32) * (1.0 / D ** 0.5)
    return values.astype(jnp.bfloat16)


def block_scale(key, shape, split, low, largest):
    loudness = 1.0
    for position, blocks in split:
        draws = jax.random.uniform(jax.random.fold_in(jax.random.fold_in(key, 6), position), (blocks,), jnp.float32, low / len(split), largest / len(split))
        loudness = loudness * jnp.repeat(jnp.exp(draws), shape[position] // blocks).reshape((-1,) + (1,) * (len(shape) - 1 - position))
    return loudness


def length_profile(number_of, total, bound, skew):
    weights = [(1 << 20) // math.isqrt(rank ** skew) + 1 for rank in range(2, number_of + 1)]
    surplus, holding = total - bound - (number_of - 1), [1] * (number_of - 1)
    while surplus > 0:
        movable = [i for i in range(number_of - 1) if holding[i] < bound]
        pool, remaining = sum([weights[i] for i in movable]), surplus
        for i in movable:
            extra = min(bound - holding[i], max(1, remaining * weights[i] // pool), surplus)
            holding[i] = holding[i] + extra
            surplus = surplus - extra
    return np.array([bound] + holding)


def uneven(own_key, amount, total, bound, skew):
    if amount == 2:
        one = jax.random.randint(own_key, (), max(1, total - bound), min(bound, total - 1) + 1)
        return jnp.stack([one, total - one])
    tallies = jnp.asarray(length_profile(amount, total, bound, skew), jnp.int32)
    couples = (amount - 1) // 2
    source_of, sink = tallies[1:1 + 2 * couples:2], tallies[2:2 + 2 * couples:2]
    margin = jnp.minimum(source_of - 1, bound - sink)
    moved = jax.random.randint(jax.random.fold_in(own_key, 1), (couples,), 0, 1 << 20) % (margin + 1)
    tallies = tallies.at[1:1 + 2 * couples:2].set(source_of - moved).at[2:2 + 2 * couples:2].set(sink + moved)
    return tallies[jax.random.permutation(jax.random.fold_in(own_key, 2), amount)]


def centred(own_key, extent, spread, reach, shards=(), kind=jnp.bfloat16):
    loudness = block_scale(own_key, extent, shards, -0.22, 0.18) if shards else 1.0
    entries = jax.random.normal(own_key, extent, jnp.float32) * spread * loudness
    return jnp.minimum(jnp.maximum(entries, -reach), reach).astype(kind)


def setup_inputs(seed: int = 0) -> dict:
    streams_of = jax.random.split(jax.random.key(seed), 10)
    return {
        "hidden_in": centred(streams_of[0], (TOKENS, D), 0.5, 4.0, ((0, 8), (1, 4))),
        "segments": jnp.searchsorted(jnp.cumsum(uneven(streams_of[1], max(TOKENS // 32, 4), TOKENS, TOKENS // 2, 2)), jnp.arange(TOKENS), side="right").astype(jnp.int32),
        "attn_gain": jnp.clip(1.0 + 0.18 * jax.random.normal(streams_of[2], (D,), jnp.float32), 0.1, 1.9),
        "query_weight": draw_query_weight(jax.random.fold_in(streams_of[9], 71), 0),
        "key_weight": centred(streams_of[4], (D, KVH * HS), D ** -0.5, 0.046875, ((0, 4), (1, 2))),
        "value_weight": centred(streams_of[5], (D, KVH * HS), D ** -0.5, 0.046875, ((0, 4), (1, 2))),
        "output_weight": centred(streams_of[6], (QH * HS, D), (QH * HS // 16) ** -0.5, 0.1875, ((0, 8), (1, 4))),
        "ffn_gain": jnp.clip(1.0 + 0.18 * jax.random.normal(streams_of[7], (D,), jnp.float32), 0.1, 1.9),
        "gate_weight": centred(streams_of[8], (D, G), D ** -0.5, 0.046875, ((0, 4), (1, 8))),
    }


EPS = 1e-05
THETA = 500000.0

def rms_scale(values, gain):
    mean_sq = lax.optimization_barrier(jnp.mean(values * values, axis=-1, keepdims=True))
    return values * lax.rsqrt(mean_sq + EPS) * gain.astype(jnp.float32)[None, :]

def positions(segments):
    count = segments.shape[0]
    same = segments[:, None] == segments[None, :]
    rows = jnp.arange(count, dtype=jnp.int32)
    earlier = rows[:, None] > rows[None, :]
    return lax.optimization_barrier(jnp.sum(jnp.where(same & earlier, 1.0, 0.0).astype(jnp.float32), axis=1))

def rotate(values, places, first_col):
    count, cols = values.shape
    pair_col = (first_col + 2 * jnp.arange(cols // 2, dtype=jnp.int32)) % HS
    freq = jnp.power(jnp.float32(THETA), -pair_col.astype(jnp.float32) / jnp.float32(HS))
    angle = places[:, None] * freq[None, :]
    paired = values.reshape(count, cols // 2, 2)
    first = paired[:, :, 0]
    second = paired[:, :, 1]
    cosine = jnp.cos(angle)
    sine = jnp.sin(angle)
    out = jnp.stack([first * cosine - second * sine, first * sine + second * cosine], axis=-1)
    return out.reshape(count, cols)

def reference(hidden_in, segments, attn_gain, query_weight, key_weight, value_weight, output_weight, ffn_gain, gate_weight):
    xin = hidden_in.astype(jnp.float32)
    normed = rms_scale(xin, attn_gain).astype(jnp.bfloat16)
    qraw = jnp.dot(normed, query_weight, preferred_element_type=jnp.float32)
    kraw = jnp.dot(normed, key_weight, preferred_element_type=jnp.float32)
    vraw = jnp.dot(normed, value_weight, preferred_element_type=jnp.float32)
    places = positions(segments)
    queries = rotate(qraw, places, 0).astype(jnp.bfloat16)
    keys = rotate(kraw, places, 0).astype(jnp.bfloat16)
    values = vraw.astype(jnp.bfloat16)
    group = QH // KVH
    q_heads = queries.reshape(TOKENS, QH, HS).astype(jnp.float32)
    k_heads = jnp.repeat(keys.reshape(TOKENS, KVH, HS), group, axis=1).astype(jnp.float32)
    v_heads = jnp.repeat(values.reshape(TOKENS, KVH, HS), group, axis=1).astype(jnp.float32)
    rows = jnp.arange(TOKENS, dtype=jnp.int32)
    allowed = (segments[:, None] == segments[None, :]) & (rows[None, :] <= rows[:, None])
    scores = jnp.einsum('qhd,khd->hqk', q_heads, k_heads) / jnp.sqrt(jnp.float32(HS))
    scores = jnp.where(allowed[None, :, :], scores, jnp.float32(-1e+30))
    top = lax.optimization_barrier(jnp.max(scores, axis=-1, keepdims=True))
    expo = jnp.exp(scores - top)
    probs = (expo / lax.optimization_barrier(jnp.sum(expo, axis=-1, keepdims=True))).astype(jnp.bfloat16)
    mixed = jnp.einsum('hqk,khd->qhd', probs.astype(jnp.float32), v_heads)
    mixed = mixed.reshape(TOKENS, QH * HS).astype(jnp.bfloat16)
    resid = xin + jnp.dot(mixed, output_weight, preferred_element_type=jnp.float32)
    ffn_in = rms_scale(resid, ffn_gain).astype(jnp.bfloat16)
    return jnp.dot(ffn_in, gate_weight, preferred_element_type=jnp.float32).astype(jnp.bfloat16)
```

```python
import functools
import math

import jax
import jax.numpy as jnp
from jax import lax
from jax.experimental import pallas as pl
from jax.experimental.pallas import tpu as pltpu
from jax.sharding import PartitionSpec as P

QH = 128
KVH = 8
HS = 128


EPS = 1e-05
THETA = 500000.0


def positions(segments):
    count = segments.shape[0]
    same = segments[:, None] == segments[None, :]
    rows = jnp.arange(count, dtype=jnp.int32)
    earlier = rows[:, None] > rows[None, :]
    return jnp.sum(jnp.where(same & earlier, 1.0, 0.0).astype(jnp.float32), axis=1)


def rotate(values, places, first_col):
    count, cols = values.shape
    pair_col = (first_col + 2 * jnp.arange(cols // 2, dtype=jnp.int32)) % HS
    freq = jnp.power(jnp.float32(THETA), -pair_col.astype(jnp.float32) / jnp.float32(HS))
    angle = places[:, None] * freq[None, :]
    paired = values.reshape(count, cols // 2, 2)
    first = paired[:, :, 0]
    second = paired[:, :, 1]
    cosine = jnp.cos(angle)
    sine = jnp.sin(angle)
    out = jnp.stack([first * cosine - second * sine, first * sine + second * cosine], axis=-1)
    return out.reshape(count, cols)


def plane_rows(local, weight):
    inner = lax.all_gather(local, "gz", axis=0, tiled=True)
    return jnp.dot(
        lax.all_gather(inner, "gy", axis=0, tiled=True), weight, preferred_element_type=jnp.float32
    )


def shards(
    hidden_in,
    segments,
    attn_gain,
    query_weight,
    key_weight,
    value_weight,
    output_weight,
    ffn_gain,
    gate_weight,
):
    width = hidden_in.shape[1] * lax.axis_size("gx")
    plane = lax.axis_index(("gy", "gz"))
    row_index = lax.axis_index("gy")
    xin = hidden_in.astype(jnp.float32)
    square_sum = lax.psum(jnp.sum(xin * xin, axis=1), "gx")
    normed = (xin * lax.rsqrt(square_sum / width + EPS)[:, None] * attn_gain[None, :]).astype(
        jnp.bfloat16
    )
    q_cols = query_weight.shape[1]
    k_cols = key_weight.shape[1]
    joined = jnp.concatenate([query_weight, key_weight, value_weight], axis=1)
    projected = plane_rows(normed, joined)
    q_part = projected[:, :q_cols]
    k_part = projected[:, q_cols : q_cols + k_cols]
    v_part = projected[:, q_cols + k_cols :]
    q_sum, k_sum, v_sum = lax.psum((q_part, k_part, v_part), "gx")
    places = positions(segments)
    queries = rotate(q_sum, places, plane * q_cols).astype(jnp.bfloat16)
    key_cols = rotate(k_sum, places, row_index * k_cols).astype(jnp.bfloat16)
    value_cols = v_sum.astype(jnp.bfloat16)
    held_heads = k_cols // HS
    first_head = row_index * held_heads
    count = key_cols.shape[0]
    local_heads = q_cols // HS
    group = QH // KVH
    needed = (plane * local_heads + jnp.arange(local_heads, dtype=jnp.int32)) // group - first_head
    select = (needed[:, None] == jnp.arange(held_heads, dtype=jnp.int32)[None, :]).astype(
        jnp.bfloat16
    )
    key_heads = jnp.einsum(
        "tkd,jk->tjd",
        key_cols.reshape(count, held_heads, HS),
        select,
        preferred_element_type=jnp.float32,
    ).astype(jnp.bfloat16)
    value_heads = jnp.einsum(
        "tkd,jk->tjd",
        value_cols.reshape(count, held_heads, HS),
        select,
        preferred_element_type=jnp.float32,
    ).astype(jnp.bfloat16)
    query_heads = queries.reshape(count, local_heads, HS)
    rows = jnp.arange(count, dtype=jnp.int32)
    allowed = (segments[:, None] == segments[None, :]) & (rows[None, :] <= rows[:, None])
    scores = jnp.einsum(
        "qhd,khd->hqk", query_heads, key_heads, preferred_element_type=jnp.float32
    ) / jnp.sqrt(jnp.float32(HS))
    scores = jnp.where(allowed[None, :, :], scores, jnp.float32(-1e30))
    top = jnp.max(scores, axis=-1, keepdims=True)
    expo = jnp.exp(scores - top)
    probs = (expo / jnp.sum(expo, axis=-1, keepdims=True)).astype(jnp.bfloat16)
    mixed = jnp.einsum("hqk,khd->qhd", probs, value_heads, preferred_element_type=jnp.float32)
    mixed = mixed.reshape(count, q_cols).astype(jnp.bfloat16)
    attended = lax.psum_scatter(
        jnp.dot(mixed, output_weight, preferred_element_type=jnp.float32),
        ("gy", "gz"),
        scatter_dimension=0,
        tiled=True,
    )
    resid = xin + attended
    resid_sum = lax.psum(jnp.sum(resid * resid, axis=1), "gx")
    ffn_in = (resid * lax.rsqrt(resid_sum / width + EPS)[:, None] * ffn_gain[None, :]).astype(
        jnp.bfloat16
    )
    gate_part = plane_rows(ffn_in, gate_weight)
    return lax.psum_scatter(gate_part, "gx", scatter_dimension=0, tiled=True).astype(jnp.bfloat16)


MESH = pl.DeviceIdType.MESH
F32 = jnp.float32
BF16 = jnp.bfloat16
LANES = 128


def fold(values):
    total = values[:, :LANES]
    for at in range(LANES, values.shape[1], LANES):
        total = total + values[:, at : at + LANES]
    return total


def block_kernel(
    cfg,
    hidden,
    seg_far,
    attn_gain_far,
    wq,
    wk,
    wv,
    wo,
    ffn_gain_far,
    wg,
    out,
    seg,
    attn_gain,
    ffn_gain,
    q_buf,
    kv_buf,
    o_buf,
    g_buf,
    x_in,
    x_f,
    x_b,
    q_send,
    q_recv,
    s_send,
    s_recv,
    mix,
    o_send,
    o_recv,
    y_buf,
    g_send,
    g_recv,
    r_send,
    r_recv,
    acc,
    inv,
    t_send,
    t_recv,
    t_all,
    w_sem,
    own_sem,
    x_ss,
    x_rs,
    q_ss,
    q_rs,
    s_ss,
    s_rs,
    m_ss,
    m_rs,
    o_ss,
    o_rs,
    y_ss,
    y_rs,
    g_ss,
    g_rs,
    r_ss,
    r_rs,
    t_ss,
    t_rs,
    u_ss,
    u_rs,
):
    n, ny, nz, width, tile, chunks = cfg
    planes = ny * nz
    gx = lax.axis_index("gx")
    gy = lax.axis_index("gy")
    gz = lax.axis_index("gz")
    plane = gy * nz + gz
    rows, depth = x_f.shape
    q_cols = q_buf.shape[1]
    part = q_send.shape[2]
    g_held = g_buf.shape[1]
    g_last = q_cols - g_held
    g_cols = wg.shape[1]
    strip = o_send.shape[2]
    block = rows // n

    near = sorted(
        [(dy, dz) for dy in range(ny) for dz in range(nz)],
        key=lambda at: (min(at[1], nz - at[1]), at[1], at[0]),
    )
    near_row = [(dx, dc) for dx in range(n // 2) for dc in range(2)]

    def plane_at(d, sign=1):
        dy, dz = near[d]
        return lax.rem(gy + sign * dy + ny, ny) * nz + lax.rem(gz + sign * dz + nz, nz)

    def row_at(d, sign=1):
        dx, dc = near_row[d]
        return lax.rem(gx // 2 + sign * dx + n // 2, n // 2) * 2 + lax.rem(gx + sign * dc + 2, 2)

    def in_plane(d):
        other = plane_at(d)
        return (gx, other // nz, lax.rem(other, nz))

    def in_row(d):
        return (row_at(d), gy, gz)

    loads = []

    def load(src, dst):
        copy = pltpu.make_async_copy(src, dst, w_sem.at[len(loads)])
        loads.append(copy)
        copy.start()
        return copy

    def load_rows(src, dst, pieces):
        step = dst.shape[0] // pieces
        return [
            load(src.at[pl.ds(i * step, step), :], dst.at[pl.ds(i * step, step), :])
            for i in range(pieces)
        ]

    barrier = pltpu.get_barrier_semaphore()
    for d in range(1, planes):
        pl.semaphore_signal(barrier, inc=1, device_id=in_plane(d), device_id_type=MESH)
    for d in range(1, n):
        pl.semaphore_signal(barrier, inc=1, device_id=in_row(d), device_id_type=MESH)
    small = [
        pltpu.make_async_copy(src, dst, own_sem.at[i])
        for i, (src, dst) in enumerate(
            (
                (hidden, x_in.at[plane]),
                (seg_far, seg),
                (attn_gain_far, attn_gain),
                (ffn_gain_far, ffn_gain),
            )
        )
    ]
    for copy in small:
        copy.start()
    for copy in small:
        copy.wait()
    head_at = pl.ds(pl.multiple_of(gz * HS, HS), HS)
    first = [
        load(wk.at[:, head_at], kv_buf.at[:, pl.ds(0, HS)]),
        load(wv.at[:, head_at], kv_buf.at[:, pl.ds(HS, HS)]),
    ] + load_rows(wq, q_buf, 4)
    second = load_rows(wo, o_buf, 4)
    third = load_rows(wg.at[:, pl.ds(0, g_held)], g_buf, 4)

    mine_f = x_in[plane].astype(F32)
    t_send[...] = fold(mine_f * mine_f)
    pl.semaphore_wait(barrier, planes + n - 2)

    def remote(src, dst, ss, rs, device):
        return pltpu.make_async_remote_copy(
            src_ref=src, dst_ref=dst, send_sem=ss, recv_sem=rs, device_id=device, device_id_type=MESH
        )

    sent = []

    def send(*what):
        copy = remote(*what)
        copy.start()
        sent.append(copy)

    order = list(range(1, planes))
    far = order[::-1]
    row = list(range(1, n))
    far_row = row[::-1]
    for d in far:
        send(x_in.at[plane], x_in.at[plane], x_ss.at[d], x_rs.at[d], in_plane(d))
    for d in far_row:
        send(t_send, t_recv.at[d], t_ss.at[d], t_rs.at[d], in_row(d))

    across = jnp.broadcast_to(seg[...].astype(F32), (rows, rows))
    down_i = lax.broadcasted_iota(jnp.int32, (rows, rows), 0)
    across_i = lax.broadcasted_iota(jnp.int32, (rows, rows), 1)
    down = jnp.sum(jnp.where(down_i == across_i, across, 0.0), axis=1, keepdims=True)
    same = across == down
    places = jnp.sum(jnp.where(same & (down_i > across_i), 1.0, 0.0), axis=1, keepdims=True)
    bias = jnp.where(same & (across_i <= down_i), 0.0, -1e30)
    lane = lax.broadcasted_iota(jnp.int32, (rows, HS), 1)
    odd = lax.rem(lane, 2)
    freq = jnp.exp((lane - odd).astype(F32) * F32(-math.log(THETA) / HS))
    angle = places * freq
    cosine = jnp.cos(angle)
    sine = jnp.sin(angle)
    sine = jnp.where(odd == 0, -sine, sine)

    inv[...] = 1.0 / (ffn_gain[...] * ffn_gain[...])
    square = t_send[...]
    for d in row:
        remote(t_send, t_recv.at[d], t_ss.at[d], t_rs.at[d], in_row(d)).wait_recv()
        square = square + t_recv[d]
    t_all[plane] = jnp.broadcast_to(
        lax.rsqrt(jnp.sum(square, axis=1, keepdims=True) / width + EPS), square.shape
    )
    for d in far:
        send(t_all.at[plane], t_all.at[plane], u_ss.at[d], u_rs.at[d], in_plane(d))
    for d in order:
        source = plane_at(d, -1)
        remote(t_all.at[plane], t_all.at[source], u_ss.at[d], u_rs.at[d], in_plane(d)).wait_recv()
        remote(x_in.at[plane], x_in.at[source], x_ss.at[d], x_rs.at[d], in_plane(d)).wait_recv()
    local_rows = rows // planes
    for p in range(planes):
        piece = x_in[p].astype(F32)
        x_f[p * local_rows : (p + 1) * local_rows, :] = piece
        acc[p * local_rows : (p + 1) * local_rows, :] = piece * t_all[p][:, :1]
    for at in range(0, depth, part):
        x_b[:, at : at + part] = (acc[:, at : at + part] * attn_gain[:, at : at + part]).astype(BF16)

    for copy in first:
        copy.wait()
    x_all = x_b[...]
    s_send[...] = jnp.dot(x_all, kv_buf[...], preferred_element_type=F32)
    for d in far_row:
        send(s_send, s_recv.at[d], s_ss.at[d], s_rs.at[d], in_row(d))
    for d in far_row + [0]:
        base = row_at(d) * part

        for t in range(part // tile):
            at = pl.multiple_of(base + t * tile, tile)
            to = t * tile
            q_send[d, :, pl.ds(to, tile)] = jnp.dot(
                x_b[...], q_buf[:, pl.ds(at, tile)], preferred_element_type=F32
            )

        if d:
            send(q_send.at[d], q_recv.at[d], q_ss.at[d], q_rs.at[d], in_row(d))
    fourth = load_rows(wg.at[:, pl.ds(g_held, q_cols)], q_buf, 4)

    shared = s_send[...]
    for d in range(1, n):
        remote(s_send, s_recv.at[d], s_ss.at[d], s_rs.at[d], in_row(d)).wait_recv()
        shared = shared + s_recv[d]

    def turn(values, cosine, sine):
        parity = lax.rem(lax.broadcasted_iota(jnp.int32, values.shape, 1), 2)
        partner = jnp.where(
            parity == 0, pltpu.roll(values, HS - 1, 1), pltpu.roll(values, 1, 1)
        )
        return (values * cosine + partner * sine).astype(BF16)

    keys = turn(shared[:, :HS], cosine, sine)
    values = shared[:, HS:].astype(BF16)
    heads = part // HS
    total = q_send[0]
    for d in range(1, n):
        remote(q_send.at[d], q_recv.at[d], q_ss.at[d], q_rs.at[d], in_row(d)).wait_recv()
        total = total + q_recv[d]
    stacked = jnp.concatenate([total[:, h * HS : (h + 1) * HS] for h in range(heads)], axis=0)
    queries = turn(
        stacked,
        jnp.concatenate([cosine] * heads, axis=0),
        jnp.concatenate([sine] * heads, axis=0),
    )
    scores = lax.dot_general(queries, keys, (((1,), (1,)), ((), ())), preferred_element_type=F32)
    scores = scores * F32(1.0 / math.sqrt(HS)) + jnp.concatenate([bias] * heads, axis=0)
    top = jnp.max(scores, axis=1, keepdims=True)
    expo = jnp.exp(scores - top)
    probs = (expo / jnp.sum(expo, axis=1, keepdims=True)).astype(BF16)
    mixed = jnp.dot(probs, values, preferred_element_type=F32).astype(BF16)
    mix[gx] = jnp.concatenate([mixed[h * rows : (h + 1) * rows] for h in range(heads)], axis=1)
    for d in far_row:
        send(mix.at[gx], mix.at[gx], m_ss.at[d], m_rs.at[d], in_row(d))
    for copy in second:
        copy.wait()

    def out_part(g, at):
        rows_at = pl.ds(pl.multiple_of(g * part, part), part)
        return jnp.dot(mix[g], o_buf[rows_at, pl.ds(at, tile)], preferred_element_type=F32)

    def mixed_from(d):
        source = row_at(d, -1)
        remote(mix.at[gx], mix.at[source], m_ss.at[d], m_rs.at[d], in_row(d)).wait_recv()
        return source

    for t in range(depth // tile):
        at = t * tile
        acc[:, pl.ds(at, tile)] = out_part(gx, at)

    near_by = mixed_from(1)

    for t in range(depth // tile):
        at = t * tile
        acc[:, pl.ds(at, tile)] += out_part(near_by, at)

    rest = [mixed_from(d) for d in row[1:]]
    for d in far + [0]:
        base = plane_at(d) * strip

        for t in range(strip // tile):
            at = pl.multiple_of(base + t * tile, tile)
            to = t * tile
            got = acc[:, pl.ds(at, tile)]
            for g in rest:
                got = got + out_part(g, at)
            o_send[d, :, pl.ds(to, tile)] = got.astype(BF16)

        if d:
            send(o_send.at[d], o_recv.at[d], o_ss.at[d], o_rs.at[d], in_plane(d))
    fifth = [
        load(
            wg.at[pl.ds(i * q_cols, q_cols), pl.ds(g_cols - g_last, g_last)],
            o_buf.at[:, pl.ds(i * g_last, g_last)],
        )
        for i in range(2)
    ]
    mine = pl.ds(pl.multiple_of(plane * strip, strip), strip)
    resid = x_f[:, mine] + o_send[0].astype(F32)
    for d in order:
        remote(o_send.at[d], o_recv.at[d], o_ss.at[d], o_rs.at[d], in_plane(d)).wait_recv()
        resid = resid + o_recv[d].astype(F32)
    y_buf[plane] = (resid * ffn_gain[:, mine]).astype(BF16)
    for d in far:
        send(y_buf.at[plane], y_buf.at[plane], y_ss.at[d], y_rs.at[d], in_plane(d))
    for copy in third + fourth + fifth:
        copy.wait()

    def gate_part(p, to):
        if to < g_held:
            held, at, first_row = g_buf, to, p * strip
        elif to < g_held + q_cols:
            held, at, first_row = q_buf, to - g_held, p * strip
        else:
            half = planes // 2
            held, first_row = o_buf, lax.rem(p, half) * strip
            at = pl.multiple_of(p // half * g_last + (to - g_held - q_cols), tile)
        rows_at = pl.ds(pl.multiple_of(first_row, strip), strip)
        return jnp.dot(y_buf[p], held[rows_at, pl.ds(at, tile)], preferred_element_type=F32)

    def squared(p):
        piece = y_buf[p].astype(F32)
        return fold(piece * piece * inv[:, pl.ds(pl.multiple_of(p * strip, strip), strip)])

    squares = squared(plane)
    passes = [[0]] + [[d] for d in order[: planes // 2 - 1]]
    left = order[planes // 2 - 1 :]
    passes += [left[:2]]
    left = left[2:]

    def arrive(d):
        if d == 0:
            return plane
        source = plane_at(d, -1)
        remote(y_buf.at[plane], y_buf.at[source], y_ss.at[d], y_rs.at[d], in_plane(d)).wait_recv()
        return source

    for number, group in enumerate(passes):
        sources = [arrive(d) for d in group]
        for to in range(0, g_cols, tile):
            got = gate_part(sources[0], to)
            for p in sources[1:]:
                got = got + gate_part(p, to)
            if number:
                got = got + acc[:, pl.ds(to, tile)]
            acc[:, pl.ds(to, tile)] = got

        if number:
            for p in sources:
                squares = squares + squared(p)

    sources = [arrive(d) for d in left]
    for p in sources:
        squares = squares + squared(p)
    for g in range(n):
        r_send[g] = squares[g * block : (g + 1) * block, :]
    for d in far_row:
        send(r_send.at[row_at(d)], r_recv.at[d], r_ss.at[d], r_rs.at[d], in_row(d))

    span = g_send.shape[3]
    for c in range(chunks):
        for to in range(0, span, tile):
            got = acc[:, pl.ds(c * span + to, tile)]
            for p in sources:
                got = got + gate_part(p, c * span + to)
            for g in range(n):
                g_send[c, g, :, pl.ds(to, tile)] = got[g * block : (g + 1) * block].astype(BF16)

        for d in far_row:
            send(
                g_send.at[c, row_at(d)],
                g_recv.at[c, d],
                g_ss.at[c, d],
                g_rs.at[c, d],
                in_row(d),
            )
    square = r_send[gx]
    for d in range(1, n):
        remote(r_send.at[0], r_recv.at[d], r_ss.at[d], r_rs.at[d], in_row(d)).wait_recv()
        square = square + r_recv[d]
    scale = lax.rsqrt(jnp.sum(square, axis=1, keepdims=True) / width + EPS)
    for c in range(chunks):
        got = g_send[c, gx].astype(F32)
        for d in range(1, n):
            remote(
                g_send.at[c, 0], g_recv.at[c, d], g_ss.at[c, d], g_rs.at[c, d], in_row(d)
            ).wait_recv()
            got = got + g_recv[c, d].astype(F32)
        out[:, c * span : (c + 1) * span] = (got * scale).astype(BF16)
    for copy in sent:
        copy.wait_send()


def fused(
    sizes,
    hidden_in,
    segments,
    attn_gain,
    query_weight,
    key_weight,
    value_weight,
    output_weight,
    ffn_gain,
    gate_weight,
):
    n, ny, nz = sizes
    planes = ny * nz
    rows = segments.shape[0]
    local_rows, depth = hidden_in.shape
    q_cols = query_weight.shape[1]
    g_cols = gate_weight.shape[1]
    part = q_cols // n
    strip = depth // planes
    block = rows // n
    tile = 512
    chunks = 4
    span = g_cols // chunks
    vmem = pltpu.VMEM
    dma = pltpu.SemaphoreType.DMA
    kernel = functools.partial(
        block_kernel, (n, ny, nz, float(depth * n), tile, chunks)
    )
    whole = pl.BlockSpec(memory_space=pltpu.VMEM)
    far = pl.BlockSpec(memory_space=pltpu.HBM)
    return pl.pallas_call(
        kernel,
        out_shape=pltpu.VMEM((block, g_cols), BF16),
        in_specs=[far] * 9,
        out_specs=whole,
        scratch_shapes=[
            vmem((1, rows), jnp.int32),
            vmem((1, depth), F32),
            vmem((1, depth), F32),
            vmem((depth, q_cols), BF16),
            vmem((depth, 2 * HS), BF16),
            vmem((q_cols, depth), BF16),
            vmem((depth, q_cols * 3 // 4), BF16),
            vmem((planes, local_rows, depth), BF16),
            vmem((rows, depth), F32),
            vmem((rows, depth), BF16),
            vmem((n, rows, part), F32),
            vmem((n, rows, part), F32),
            vmem((rows, 2 * HS), F32),
            vmem((n, rows, 2 * HS), F32),
            vmem((n, rows, part), BF16),
            vmem((planes, rows, strip), BF16),
            vmem((planes, rows, strip), BF16),
            vmem((planes, rows, strip), BF16),
            vmem((chunks, n, block, span), BF16),
            vmem((chunks, n, block, span), BF16),
            vmem((n, block, LANES), F32),
            vmem((n, block, LANES), F32),
            vmem((rows, depth), F32),
            vmem((1, depth), F32),
            vmem((local_rows, LANES), F32),
            vmem((n, local_rows, LANES), F32),
            vmem((planes, local_rows, LANES), F32),
            dma((20,)),
            dma((4,)),
            dma((planes,)),
            dma((planes,)),
            dma((n,)),
            dma((n,)),
            dma((n,)),
            dma((n,)),
            dma((n,)),
            dma((n,)),
            dma((planes,)),
            dma((planes,)),
            dma((planes,)),
            dma((planes,)),
            dma((chunks, n)),
            dma((chunks, n)),
            dma((n,)),
            dma((n,)),
            dma((n,)),
            dma((n,)),
            dma((planes,)),
            dma((planes,)),
        ],
        compiler_params=pltpu.CompilerParams(
            collective_id=0, has_side_effects=True, vmem_limit_bytes=52 * 1024 * 1024
        ),
    )(
        *(
            pltpu.with_memory_space_constraint(array, pltpu.HBM)
            for array in (
                hidden_in,
                segments.reshape(1, rows),
                attn_gain.reshape(1, depth),
                query_weight,
                key_weight,
                value_weight,
                output_weight,
                ffn_gain.reshape(1, depth),
                gate_weight,
            )
        )
    )


def local(sizes, *arrays):
    n, ny, nz = sizes
    planes = ny * nz
    hidden_in, segments, _, query_weight, key_weight, _, output_weight, _, gate_weight = arrays
    depth, q_cols = query_weight.shape
    fits = (
        q_cols // HS == QH // KVH
        and key_weight.shape[1] == nz * HS
        and gate_weight.shape[1] == 2 * q_cols
        and segments.shape[0] == 8 * n
        and n % 2 == 0
        and (q_cols // n) % 512 == 0
        and depth % (q_cols // n) == 0
        and (depth // planes) % 512 == 0
        and depth == 2 * q_cols
        and depth * q_cols * 6 <= 56 * 1024 * 1024
    )
    return fused(sizes, *arrays) if fits else shards(*arrays)


def solution(mesh):
    return jax.shard_map(
        functools.partial(local, tuple(mesh.shape[name] for name in ("gx", "gy", "gz"))),
        mesh=mesh,
        in_specs=(
            P(("gy", "gz"), "gx"),
            P(),
            P("gx"),
            P("gx", ("gy", "gz")),
            P("gx", "gy"),
            P("gx", "gy"),
            P(("gy", "gz"), "gx"),
            P("gx"),
            P("gx", ("gy", "gz")),
        ),
        out_specs=P("gx", ("gy", "gz")),
        check_vma=False,
    )
```

```python
import functools
import math

import jax
import jax.numpy as jnp
from jax import lax
from jax.experimental import pallas as pl
from jax.experimental.pallas import tpu as pltpu
from jax.sharding import PartitionSpec as P

QH = 128
KVH = 8
HS = 128


EPS = 1e-05
THETA = 500000.0


def positions(segments):
    count = segments.shape[0]
    same = segments[:, None] == segments[None, :]
    rows = jnp.arange(count, dtype=jnp.int32)
    earlier = rows[:, None] > rows[None, :]
    return jnp.sum(jnp.where(same & earlier, 1.0, 0.0).astype(jnp.float32), axis=1)


def rotate(values, places, first_col):
    count, cols = values.shape
    pair_col = (first_col + 2 * jnp.arange(cols // 2, dtype=jnp.int32)) % HS
    freq = jnp.power(jnp.float32(THETA), -pair_col.astype(jnp.float32) / jnp.float32(HS))
    angle = places[:, None] * freq[None, :]
    paired = values.reshape(count, cols // 2, 2)
    first = paired[:, :, 0]
    second = paired[:, :, 1]
    cosine = jnp.cos(angle)
    sine = jnp.sin(angle)
    out = jnp.stack([first * cosine - second * sine, first * sine + second * cosine], axis=-1)
    return out.reshape(count, cols)


def plane_rows(local, weight):
    inner = lax.all_gather(local, "gz", axis=0, tiled=True)
    return jnp.dot(
        lax.all_gather(inner, "gy", axis=0, tiled=True), weight, preferred_element_type=jnp.float32
    )


def shards(
    hidden_in,
    segments,
    attn_gain,
    query_weight,
    key_weight,
    value_weight,
    output_weight,
    ffn_gain,
    gate_weight,
):
    width = hidden_in.shape[1] * lax.axis_size("gx")
    plane = lax.axis_index(("gy", "gz"))
    row_index = lax.axis_index("gy")
    xin = hidden_in.astype(jnp.float32)
    square_sum = lax.psum(jnp.sum(xin * xin, axis=1), "gx")
    normed = (xin * lax.rsqrt(square_sum / width + EPS)[:, None] * attn_gain[None, :]).astype(
        jnp.bfloat16
    )
    q_cols = query_weight.shape[1]
    k_cols = key_weight.shape[1]
    joined = jnp.concatenate([query_weight, key_weight, value_weight], axis=1)
    projected = plane_rows(normed, joined)
    q_part = projected[:, :q_cols]
    k_part = projected[:, q_cols : q_cols + k_cols]
    v_part = projected[:, q_cols + k_cols :]
    q_sum, k_sum, v_sum = lax.psum((q_part, k_part, v_part), "gx")
    places = positions(segments)
    queries = rotate(q_sum, places, plane * q_cols).astype(jnp.bfloat16)
    key_cols = rotate(k_sum, places, row_index * k_cols).astype(jnp.bfloat16)
    value_cols = v_sum.astype(jnp.bfloat16)
    held_heads = k_cols // HS
    first_head = row_index * held_heads
    count = key_cols.shape[0]
    local_heads = q_cols // HS
    group = QH // KVH
    needed = (plane * local_heads + jnp.arange(local_heads, dtype=jnp.int32)) // group - first_head
    select = (needed[:, None] == jnp.arange(held_heads, dtype=jnp.int32)[None, :]).astype(
        jnp.bfloat16
    )
    key_heads = jnp.einsum(
        "tkd,jk->tjd",
        key_cols.reshape(count, held_heads, HS),
        select,
        preferred_element_type=jnp.float32,
    ).astype(jnp.bfloat16)
    value_heads = jnp.einsum(
        "tkd,jk->tjd",
        value_cols.reshape(count, held_heads, HS),
        select,
        preferred_element_type=jnp.float32,
    ).astype(jnp.bfloat16)
    query_heads = queries.reshape(count, local_heads, HS)
    rows = jnp.arange(count, dtype=jnp.int32)
    allowed = (segments[:, None] == segments[None, :]) & (rows[None, :] <= rows[:, None])
    scores = jnp.einsum(
        "qhd,khd->hqk", query_heads, key_heads, preferred_element_type=jnp.float32
    ) / jnp.sqrt(jnp.float32(HS))
    scores = jnp.where(allowed[None, :, :], scores, jnp.float32(-1e30))
    top = jnp.max(scores, axis=-1, keepdims=True)
    expo = jnp.exp(scores - top)
    probs = (expo / jnp.sum(expo, axis=-1, keepdims=True)).astype(jnp.bfloat16)
    mixed = jnp.einsum("hqk,khd->qhd", probs, value_heads, preferred_element_type=jnp.float32)
    mixed = mixed.reshape(count, q_cols).astype(jnp.bfloat16)
    attended = lax.psum_scatter(
        jnp.dot(mixed, output_weight, preferred_element_type=jnp.float32),
        ("gy", "gz"),
        scatter_dimension=0,
        tiled=True,
    )
    resid = xin + attended
    resid_sum = lax.psum(jnp.sum(resid * resid, axis=1), "gx")
    ffn_in = (resid * lax.rsqrt(resid_sum / width + EPS)[:, None] * ffn_gain[None, :]).astype(
        jnp.bfloat16
    )
    gate_part = plane_rows(ffn_in, gate_weight)
    return lax.psum_scatter(gate_part, "gx", scatter_dimension=0, tiled=True).astype(jnp.bfloat16)


MESH = pl.DeviceIdType.MESH
F32 = jnp.float32
BF16 = jnp.bfloat16
LANES = 128


def fold(values):
    total = values[:, :LANES]
    for at in range(LANES, values.shape[1], LANES):
        total = total + values[:, at : at + LANES]
    return total


def block_kernel(
    cfg,
    hidden,
    seg_far,
    attn_gain_far,
    wq,
    wk,
    wv,
    wo,
    ffn_gain_far,
    wg,
    out,
    seg,
    attn_gain,
    ffn_gain,
    q_buf,
    kv_buf,
    o_buf,
    g_buf,
    x_in,
    x_f,
    x_b,
    q_send,
    q_recv,
    s_send,
    s_recv,
    mix,
    o_send,
    o_recv,
    y_buf,
    g_send,
    g_recv,
    r_send,
    r_recv,
    acc,
    inv,
    t_send,
    t_recv,
    t_all,
    w_sem,
    own_sem,
    x_ss,
    x_rs,
    q_ss,
    q_rs,
    s_ss,
    s_rs,
    m_ss,
    m_rs,
    o_ss,
    o_rs,
    y_ss,
    y_rs,
    g_ss,
    g_rs,
    r_ss,
    r_rs,
    t_ss,
    t_rs,
    u_ss,
    u_rs,
):
    n, ny, nz, width, tile, chunks = cfg
    planes = ny * nz
    gx = lax.axis_index("gx")
    gy = lax.axis_index("gy")
    gz = lax.axis_index("gz")
    plane = gy * nz + gz
    rows, depth = x_f.shape
    q_cols = q_buf.shape[1]
    part = q_send.shape[2]
    g_held = g_buf.shape[1]
    g_last = q_cols - g_held
    g_cols = wg.shape[1]
    halves, _, _, piece = o_send.shape
    strip = halves * piece
    block = rows // n

    near = sorted(
        [(dy, dz) for dy in range(ny) for dz in range(nz)],
        key=lambda at: (min(at[1], nz - at[1]), at[1], at[0]),
    )
    near_row = [(dx, dc) for dx in range(n // 2) for dc in range(2)]

    def plane_at(d, sign=1):
        dy, dz = near[d]
        return lax.rem(gy + sign * dy + ny, ny) * nz + lax.rem(gz + sign * dz + nz, nz)

    def row_at(d, sign=1):
        dx, dc = near_row[d]
        return lax.rem(gx // 2 + sign * dx + n // 2, n // 2) * 2 + lax.rem(gx + sign * dc + 2, 2)

    def in_plane(d):
        other = plane_at(d)
        return (gx, other // nz, lax.rem(other, nz))

    def in_row(d):
        return (row_at(d), gy, gz)

    loads = []

    def load(src, dst):
        copy = pltpu.make_async_copy(src, dst, w_sem.at[len(loads)])
        loads.append(copy)
        copy.start()
        return copy

    def load_rows(src, dst, pieces):
        step = dst.shape[0] // pieces
        return [
            load(src.at[pl.ds(i * step, step), :], dst.at[pl.ds(i * step, step), :])
            for i in range(pieces)
        ]

    barrier = pltpu.get_barrier_semaphore()
    for d in range(1, planes):
        pl.semaphore_signal(barrier, inc=1, device_id=in_plane(d), device_id_type=MESH)
    for d in range(1, n):
        pl.semaphore_signal(barrier, inc=1, device_id=in_row(d), device_id_type=MESH)
    small = [
        pltpu.make_async_copy(src, dst, own_sem.at[i])
        for i, (src, dst) in enumerate(
            (
                (hidden, x_in.at[plane]),
                (seg_far, seg),
                (attn_gain_far, attn_gain),
                (ffn_gain_far, ffn_gain),
            )
        )
    ]
    for copy in small:
        copy.start()
    for copy in small:
        copy.wait()
    head_at = pl.ds(pl.multiple_of(gz * HS, HS), HS)
    first = [
        load(wk.at[:, head_at], kv_buf.at[:, pl.ds(0, HS)]),
        load(wv.at[:, head_at], kv_buf.at[:, pl.ds(HS, HS)]),
    ] + load_rows(wq, q_buf, 4)

    mine_f = x_in[plane].astype(F32)
    t_send[...] = fold(mine_f * mine_f)
    pl.semaphore_wait(barrier, planes + n - 2)

    def remote(src, dst, ss, rs, device):
        return pltpu.make_async_remote_copy(
            src_ref=src, dst_ref=dst, send_sem=ss, recv_sem=rs, device_id=device, device_id_type=MESH
        )

    sent = []

    def send(*what):
        copy = remote(*what)
        copy.start()
        sent.append(copy)

    order = list(range(1, planes))
    far = order[::-1]
    row = list(range(1, n))
    far_row = row[::-1]
    for d in far:
        send(x_in.at[plane], x_in.at[plane], x_ss.at[d], x_rs.at[d], in_plane(d))
    for d in far_row:
        send(t_send, t_recv.at[d], t_ss.at[d], t_rs.at[d], in_row(d))

    second = load_rows(wo, o_buf, 4)
    third = load_rows(wg.at[:, pl.ds(0, g_held)], g_buf, 4)
    across = jnp.broadcast_to(seg[...].astype(F32), (rows, rows))
    down_i = lax.broadcasted_iota(jnp.int32, (rows, rows), 0)
    across_i = lax.broadcasted_iota(jnp.int32, (rows, rows), 1)
    down = jnp.sum(jnp.where(down_i == across_i, across, 0.0), axis=1, keepdims=True)
    same = across == down
    places = jnp.sum(jnp.where(same & (down_i > across_i), 1.0, 0.0), axis=1, keepdims=True)
    bias = jnp.where(same & (across_i <= down_i), 0.0, -1e30)
    lane = lax.broadcasted_iota(jnp.int32, (rows, HS), 1)
    odd = lax.rem(lane, 2)
    freq = jnp.exp((lane - odd).astype(F32) * F32(-math.log(THETA) / HS))
    angle = places * freq
    cosine = jnp.cos(angle)
    sine = jnp.sin(angle)
    sine = jnp.where(odd == 0, -sine, sine)

    inv[...] = 1.0 / (ffn_gain[...] * ffn_gain[...])
    square = t_send[...]
    for d in row:
        remote(t_send, t_recv.at[d], t_ss.at[d], t_rs.at[d], in_row(d)).wait_recv()
        square = square + t_recv[d]
    t_all[plane] = jnp.broadcast_to(
        lax.rsqrt(jnp.sum(square, axis=1, keepdims=True) / width + EPS), square.shape
    )
    for d in far:
        send(t_all.at[plane], t_all.at[plane], u_ss.at[d], u_rs.at[d], in_plane(d))
    for d in order:
        source = plane_at(d, -1)
        remote(t_all.at[plane], t_all.at[source], u_ss.at[d], u_rs.at[d], in_plane(d)).wait_recv()
        remote(x_in.at[plane], x_in.at[source], x_ss.at[d], x_rs.at[d], in_plane(d)).wait_recv()
    local_rows = rows // planes
    for p in range(planes):
        tokens = x_in[p].astype(F32)
        x_f[p * local_rows : (p + 1) * local_rows, :] = tokens
        acc[p * local_rows : (p + 1) * local_rows, :] = tokens * t_all[p][:, :1]
    for at in range(0, depth, part):
        x_b[:, at : at + part] = (acc[:, at : at + part] * attn_gain[:, at : at + part]).astype(BF16)

    for copy in first:
        copy.wait()
    x_all = x_b[...]
    s_send[...] = jnp.dot(x_all, kv_buf[...], preferred_element_type=F32)
    for d in far_row:
        send(s_send, s_recv.at[d], s_ss.at[d], s_rs.at[d], in_row(d))
    for d in far_row + [0]:
        base = row_at(d) * part

        for t in range(part // tile):
            at = pl.multiple_of(base + t * tile, tile)
            to = t * tile
            q_send[d, :, pl.ds(to, tile)] = jnp.dot(
                x_b[...], q_buf[:, pl.ds(at, tile)], preferred_element_type=F32
            )

        if d:
            send(q_send.at[d], q_recv.at[d], q_ss.at[d], q_rs.at[d], in_row(d))
    fourth = load_rows(wg.at[:, pl.ds(g_held, q_cols)], q_buf, 4)

    shared = s_send[...]
    for d in range(1, n):
        remote(s_send, s_recv.at[d], s_ss.at[d], s_rs.at[d], in_row(d)).wait_recv()
        shared = shared + s_recv[d]

    def turn(values, cosine, sine):
        parity = lax.rem(lax.broadcasted_iota(jnp.int32, values.shape, 1), 2)
        partner = jnp.where(
            parity == 0, pltpu.roll(values, HS - 1, 1), pltpu.roll(values, 1, 1)
        )
        return (values * cosine + partner * sine).astype(BF16)

    keys = turn(shared[:, :HS], cosine, sine)
    values = shared[:, HS:].astype(BF16)
    heads = part // HS
    total = q_send[0]
    for d in range(1, n):
        remote(q_send.at[d], q_recv.at[d], q_ss.at[d], q_rs.at[d], in_row(d)).wait_recv()
        total = total + q_recv[d]
    stacked = jnp.concatenate([total[:, h * HS : (h + 1) * HS] for h in range(heads)], axis=0)
    queries = turn(
        stacked,
        jnp.concatenate([cosine] * heads, axis=0),
        jnp.concatenate([sine] * heads, axis=0),
    )
    scores = lax.dot_general(queries, keys, (((1,), (1,)), ((), ())), preferred_element_type=F32)
    scores = scores * F32(1.0 / math.sqrt(HS)) + jnp.concatenate([bias] * heads, axis=0)
    top = jnp.max(scores, axis=1, keepdims=True)
    expo = jnp.exp(scores - top)
    probs = (expo / jnp.sum(expo, axis=1, keepdims=True)).astype(BF16)
    mixed = jnp.dot(probs, values, preferred_element_type=F32).astype(BF16)
    mix[gx] = jnp.concatenate([mixed[h * rows : (h + 1) * rows] for h in range(heads)], axis=1)
    for d in far_row:
        send(mix.at[gx], mix.at[gx], m_ss.at[d], m_rs.at[d], in_row(d))
    for copy in second:
        copy.wait()

    def out_part(g, at, size):
        rows_at = pl.ds(pl.multiple_of(g * part, part), part)
        return jnp.dot(mix[g], o_buf[rows_at, pl.ds(at, size)], preferred_element_type=F32)

    def mixed_from(d):
        source = row_at(d, -1)
        remote(mix.at[gx], mix.at[source], m_ss.at[d], m_rs.at[d], in_row(d)).wait_recv()
        return source

    for t in range(depth // tile):
        at = t * tile
        acc[:, pl.ds(at, tile)] = out_part(gx, at, tile)

    near_by = mixed_from(1)

    for t in range(depth // tile):
        at = t * tile
        acc[:, pl.ds(at, tile)] += out_part(near_by, at, tile)

    rest = [mixed_from(d) for d in row[1:]]
    for h in range(halves):
        for d in far + [0]:
            at = pl.multiple_of(plane_at(d) * strip + h * piece, piece)
            got = acc[:, pl.ds(at, piece)]
            for g in rest:
                got = got + out_part(g, at, piece)
            o_send[h, d] = got.astype(BF16)
            if d:
                send(
                    o_send.at[h, d], o_recv.at[h, d], o_ss.at[h, d], o_rs.at[h, d], in_plane(d)
                )
    fifth = [
        load(
            wg.at[pl.ds(i * q_cols, q_cols), pl.ds(g_cols - g_last, g_last)],
            o_buf.at[:, pl.ds(i * g_last, g_last)],
        )
        for i in range(2)
    ]
    def settle(h):
        mine = pl.ds(pl.multiple_of(plane * strip + h * piece, piece), piece)
        resid = x_f[:, mine] + o_send[h, 0].astype(F32)
        for d in order:
            remote(
                o_send.at[h, d], o_recv.at[h, d], o_ss.at[h, d], o_rs.at[h, d], in_plane(d)
            ).wait_recv()
            resid = resid + o_recv[h, d].astype(F32)
        y_buf[h, plane] = (resid * ffn_gain[:, mine]).astype(BF16)
        for d in far:
            send(
                y_buf.at[h, plane], y_buf.at[h, plane], y_ss.at[h, d], y_rs.at[h, d], in_plane(d)
            )

    def gate_part(h, p, to):
        first_row = p * strip + h * piece
        if to < g_held:
            held, at = g_buf, to
        elif to < g_held + q_cols:
            held, at = q_buf, to - g_held
        else:
            half = planes // 2
            held, first_row = o_buf, lax.rem(p, half) * strip + h * piece
            at = pl.multiple_of(p // half * g_last + (to - g_held - q_cols), tile)
        rows_at = pl.ds(pl.multiple_of(first_row, piece), piece)
        return jnp.dot(y_buf[h, p], held[rows_at, pl.ds(at, tile)], preferred_element_type=F32)

    def squared(h, p):
        value = y_buf[h, p].astype(F32)
        at = pl.ds(pl.multiple_of(p * strip + h * piece, piece), piece)
        return fold(value * value * inv[:, at])

    def arrive(h, d):
        if d == 0:
            return h, plane
        source = plane_at(d, -1)
        remote(
            y_buf.at[h, plane], y_buf.at[h, source], y_ss.at[h, d], y_rs.at[h, d], in_plane(d)
        ).wait_recv()
        return h, source

    def gate_pass(sources, first):
        for to in range(0, g_cols, tile):
            got = gate_part(*sources[0], to)
            for at in sources[1:]:
                got = got + gate_part(*at, to)
            if not first:
                got = got + acc[:, pl.ds(to, tile)]
            acc[:, pl.ds(to, tile)] = got

    settle(0)
    for copy in third + fourth + fifth:
        copy.wait()
    gate_pass([(0, plane)], True)
    squares = squared(0, plane)
    for h in range(1, halves):
        settle(h)
        gate_pass([(h, plane)], False)
        squares = squares + squared(h, plane)
    units = [(h, d) for h in range(halves) for d in order]
    left = units[-4:]
    sizes = [2,2,2,2,2]
    while len(units) > 4:
        size = sizes.pop(0)
        sources = [arrive(*unit) for unit in units[:size]]
        units = units[size:]
        gate_pass(sources, False)
        for at in sources:
            squares = squares + squared(*at)

    sources = [arrive(*unit) for unit in left]
    for at in sources:
        squares = squares + squared(*at)
    for g in range(n):
        r_send[g] = squares[g * block : (g + 1) * block, :]
    for d in far_row:
        send(r_send.at[row_at(d)], r_recv.at[d], r_ss.at[d], r_rs.at[d], in_row(d))

    span = g_send.shape[3]
    for c in range(chunks):
        for to in range(0, span, tile):
            got = acc[:, pl.ds(c * span + to, tile)]
            for at in sources:
                got = got + gate_part(*at, c * span + to)
            for g in range(n):
                g_send[c, g, :, pl.ds(to, tile)] = got[g * block : (g + 1) * block].astype(BF16)

        for d in far_row:
            send(
                g_send.at[c, row_at(d)],
                g_recv.at[c, d],
                g_ss.at[c, d],
                g_rs.at[c, d],
                in_row(d),
            )
    square = r_send[gx]
    for d in range(1, n):
        remote(r_send.at[0], r_recv.at[d], r_ss.at[d], r_rs.at[d], in_row(d)).wait_recv()
        square = square + r_recv[d]
    scale = lax.rsqrt(jnp.sum(square, axis=1, keepdims=True) / width + EPS)
    for c in range(chunks):
        got = g_send[c, gx].astype(F32)
        for d in range(1, n):
            remote(
                g_send.at[c, 0], g_recv.at[c, d], g_ss.at[c, d], g_rs.at[c, d], in_row(d)
            ).wait_recv()
            got = got + g_recv[c, d].astype(F32)
        out[:, c * span : (c + 1) * span] = (got * scale).astype(BF16)
    for copy in sent:
        copy.wait_send()


def fused(
    sizes,
    hidden_in,
    segments,
    attn_gain,
    query_weight,
    key_weight,
    value_weight,
    output_weight,
    ffn_gain,
    gate_weight,
):
    n, ny, nz = sizes
    planes = ny * nz
    rows = segments.shape[0]
    local_rows, depth = hidden_in.shape
    q_cols = query_weight.shape[1]
    g_cols = gate_weight.shape[1]
    part = q_cols // n
    strip = depth // planes
    block = rows // n
    tile = 512
    chunks = 4
    halves = 2
    span = g_cols // chunks
    vmem = pltpu.VMEM
    dma = pltpu.SemaphoreType.DMA
    kernel = functools.partial(
        block_kernel, (n, ny, nz, float(depth * n), tile, chunks)
    )
    whole = pl.BlockSpec(memory_space=pltpu.VMEM)
    far = pl.BlockSpec(memory_space=pltpu.HBM)
    return pl.pallas_call(
        kernel,
        out_shape=pltpu.VMEM((block, g_cols), BF16),
        in_specs=[far] * 9,
        out_specs=whole,
        scratch_shapes=[
            vmem((1, rows), jnp.int32),
            vmem((1, depth), F32),
            vmem((1, depth), F32),
            vmem((depth, q_cols), BF16),
            vmem((depth, 2 * HS), BF16),
            vmem((q_cols, depth), BF16),
            vmem((depth, q_cols * 3 // 4), BF16),
            vmem((planes, local_rows, depth), BF16),
            vmem((rows, depth), F32),
            vmem((rows, depth), BF16),
            vmem((n, rows, part), F32),
            vmem((n, rows, part), F32),
            vmem((rows, 2 * HS), F32),
            vmem((n, rows, 2 * HS), F32),
            vmem((n, rows, part), BF16),
            vmem((halves, planes, rows, strip // halves), BF16),
            vmem((halves, planes, rows, strip // halves), BF16),
            vmem((halves, planes, rows, strip // halves), BF16),
            vmem((chunks, n, block, span), BF16),
            vmem((chunks, n, block, span), BF16),
            vmem((n, block, LANES), F32),
            vmem((n, block, LANES), F32),
            vmem((rows, depth), F32),
            vmem((1, depth), F32),
            vmem((local_rows, LANES), F32),
            vmem((n, local_rows, LANES), F32),
            vmem((planes, local_rows, LANES), F32),
            dma((20,)),
            dma((4,)),
            dma((planes,)),
            dma((planes,)),
            dma((n,)),
            dma((n,)),
            dma((n,)),
            dma((n,)),
            dma((n,)),
            dma((n,)),
            dma((halves, planes)),
            dma((halves, planes)),
            dma((halves, planes)),
            dma((halves, planes)),
            dma((chunks, n)),
            dma((chunks, n)),
            dma((n,)),
            dma((n,)),
            dma((n,)),
            dma((n,)),
            dma((planes,)),
            dma((planes,)),
        ],
        compiler_params=pltpu.CompilerParams(
            collective_id=0, has_side_effects=True, vmem_limit_bytes=52 * 1024 * 1024
        ),
    )(
        *(
            pltpu.with_memory_space_constraint(array, pltpu.HBM)
            for array in (
                hidden_in,
                segments.reshape(1, rows),
                attn_gain.reshape(1, depth),
                query_weight,
                key_weight,
                value_weight,
                output_weight,
                ffn_gain.reshape(1, depth),
                gate_weight,
            )
        )
    )


def local(sizes, *arrays):
    n, ny, nz = sizes
    planes = ny * nz
    hidden_in, segments, _, query_weight, key_weight, _, output_weight, _, gate_weight = arrays
    depth, q_cols = query_weight.shape
    fits = (
        q_cols // HS == QH // KVH
        and key_weight.shape[1] == nz * HS
        and gate_weight.shape[1] == 2 * q_cols
        and segments.shape[0] == 8 * n
        and n == 4
        and (q_cols // n) % 512 == 0
        and depth % (q_cols // n) == 0
        and (depth // planes) % 512 == 0
        and depth == 2 * q_cols
        and depth * q_cols * 6 <= 56 * 1024 * 1024
    )
    return fused(sizes, *arrays) if fits else shards(*arrays)


def solution(mesh):
    return jax.shard_map(
        functools.partial(local, tuple(mesh.shape[name] for name in ("gx", "gy", "gz"))),
        mesh=mesh,
        in_specs=(
            P(("gy", "gz"), "gx"),
            P(),
            P("gx"),
            P("gx", ("gy", "gz")),
            P("gx", "gy"),
            P("gx", "gy"),
            P(("gy", "gz"), "gx"),
            P("gx"),
            P("gx", ("gy", "gz")),
        ),
        out_specs=P("gx", ("gy", "gz")),
        check_vma=False,
    )
```

```python
import functools
import math

import jax
import jax.numpy as jnp
from jax import lax
from jax.experimental import pallas as pl
from jax.experimental.pallas import tpu as pltpu
from jax.sharding import PartitionSpec as P

QH = 128
KVH = 8
HS = 128


EPS = 1e-05
THETA = 500000.0


def positions(segments):
    count = segments.shape[0]
    same = segments[:, None] == segments[None, :]
    rows = jnp.arange(count, dtype=jnp.int32)
    earlier = rows[:, None] > rows[None, :]
    return jnp.sum(jnp.where(same & earlier, 1.0, 0.0).astype(jnp.float32), axis=1)


def rotate(values, places, first_col):
    count, cols = values.shape
    pair_col = (first_col + 2 * jnp.arange(cols // 2, dtype=jnp.int32)) % HS
    freq = jnp.power(jnp.float32(THETA), -pair_col.astype(jnp.float32) / jnp.float32(HS))
    angle = places[:, None] * freq[None, :]
    paired = values.reshape(count, cols // 2, 2)
    first = paired[:, :, 0]
    second = paired[:, :, 1]
    cosine = jnp.cos(angle)
    sine = jnp.sin(angle)
    out = jnp.stack([first * cosine - second * sine, first * sine + second * cosine], axis=-1)
    return out.reshape(count, cols)


def plane_rows(local, weight):
    inner = lax.all_gather(local, "gz", axis=0, tiled=True)
    return jnp.dot(
        lax.all_gather(inner, "gy", axis=0, tiled=True), weight, preferred_element_type=jnp.float32
    )


def shards(
    hidden_in,
    segments,
    attn_gain,
    query_weight,
    key_weight,
    value_weight,
    output_weight,
    ffn_gain,
    gate_weight,
):
    width = hidden_in.shape[1] * lax.axis_size("gx")
    plane = lax.axis_index(("gy", "gz"))
    row_index = lax.axis_index("gy")
    xin = hidden_in.astype(jnp.float32)
    square_sum = lax.psum(jnp.sum(xin * xin, axis=1), "gx")
    normed = (xin * lax.rsqrt(square_sum / width + EPS)[:, None] * attn_gain[None, :]).astype(
        jnp.bfloat16
    )
    q_cols = query_weight.shape[1]
    k_cols = key_weight.shape[1]
    joined = jnp.concatenate([query_weight, key_weight, value_weight], axis=1)
    projected = plane_rows(normed, joined)
    q_part = projected[:, :q_cols]
    k_part = projected[:, q_cols : q_cols + k_cols]
    v_part = projected[:, q_cols + k_cols :]
    q_sum, k_sum, v_sum = lax.psum((q_part, k_part, v_part), "gx")
    places = positions(segments)
    queries = rotate(q_sum, places, plane * q_cols).astype(jnp.bfloat16)
    key_cols = rotate(k_sum, places, row_index * k_cols).astype(jnp.bfloat16)
    value_cols = v_sum.astype(jnp.bfloat16)
    held_heads = k_cols // HS
    first_head = row_index * held_heads
    count = key_cols.shape[0]
    local_heads = q_cols // HS
    group = QH // KVH
    needed = (plane * local_heads + jnp.arange(local_heads, dtype=jnp.int32)) // group - first_head
    select = (needed[:, None] == jnp.arange(held_heads, dtype=jnp.int32)[None, :]).astype(
        jnp.bfloat16
    )
    key_heads = jnp.einsum(
        "tkd,jk->tjd",
        key_cols.reshape(count, held_heads, HS),
        select,
        preferred_element_type=jnp.float32,
    ).astype(jnp.bfloat16)
    value_heads = jnp.einsum(
        "tkd,jk->tjd",
        value_cols.reshape(count, held_heads, HS),
        select,
        preferred_element_type=jnp.float32,
    ).astype(jnp.bfloat16)
    query_heads = queries.reshape(count, local_heads, HS)
    rows = jnp.arange(count, dtype=jnp.int32)
    allowed = (segments[:, None] == segments[None, :]) & (rows[None, :] <= rows[:, None])
    scores = jnp.einsum(
        "qhd,khd->hqk", query_heads, key_heads, preferred_element_type=jnp.float32
    ) / jnp.sqrt(jnp.float32(HS))
    scores = jnp.where(allowed[None, :, :], scores, jnp.float32(-1e30))
    top = jnp.max(scores, axis=-1, keepdims=True)
    expo = jnp.exp(scores - top)
    probs = (expo / jnp.sum(expo, axis=-1, keepdims=True)).astype(jnp.bfloat16)
    mixed = jnp.einsum("hqk,khd->qhd", probs, value_heads, preferred_element_type=jnp.float32)
    mixed = mixed.reshape(count, q_cols).astype(jnp.bfloat16)
    attended = lax.psum_scatter(
        jnp.dot(mixed, output_weight, preferred_element_type=jnp.float32),
        ("gy", "gz"),
        scatter_dimension=0,
        tiled=True,
    )
    resid = xin + attended
    resid_sum = lax.psum(jnp.sum(resid * resid, axis=1), "gx")
    ffn_in = (resid * lax.rsqrt(resid_sum / width + EPS)[:, None] * ffn_gain[None, :]).astype(
        jnp.bfloat16
    )
    gate_part = plane_rows(ffn_in, gate_weight)
    return lax.psum_scatter(gate_part, "gx", scatter_dimension=0, tiled=True).astype(jnp.bfloat16)


MESH = pl.DeviceIdType.MESH
F32 = jnp.float32
BF16 = jnp.bfloat16
LANES = 128


def fold(values):
    total = values[:, :LANES]
    for at in range(LANES, values.shape[1], LANES):
        total = total + values[:, at : at + LANES]
    return total


def block_kernel(
    cfg,
    hidden,
    seg_far,
    attn_gain_far,
    wq,
    wk,
    wv,
    wo,
    ffn_gain_far,
    wg,
    out,
    seg,
    attn_gain,
    ffn_gain,
    q_buf,
    kv_buf,
    o_buf,
    g_buf,
    x_in,
    x_f,
    x_b,
    q_send,
    q_recv,
    s_send,
    s_recv,
    mix,
    o_send,
    o_recv,
    y_buf,
    g_send,
    g_recv,
    r_send,
    r_recv,
    acc,
    inv,
    t_send,
    t_recv,
    t_all,
    w_sem,
    own_sem,
    x_ss,
    x_rs,
    q_ss,
    q_rs,
    s_ss,
    s_rs,
    m_ss,
    m_rs,
    o_ss,
    o_rs,
    y_ss,
    y_rs,
    g_ss,
    g_rs,
    r_ss,
    r_rs,
    t_ss,
    t_rs,
    u_ss,
    u_rs,
):
    n, ny, nz, width, tile, chunks = cfg
    planes = ny * nz
    gx = lax.axis_index("gx")
    gy = lax.axis_index("gy")
    gz = lax.axis_index("gz")
    plane = gy * nz + gz
    rows, depth = x_f.shape
    q_cols = q_buf.shape[1]
    part = q_send.shape[2]
    g_held = g_buf.shape[1]
    g_last = q_cols - g_held
    g_cols = wg.shape[1]
    halves, _, _, piece = o_send.shape
    strip = halves * piece
    block = rows // n

    near = sorted(
        [(dy, dz) for dy in range(ny) for dz in range(nz)],
        key=lambda at: (min(at[1], nz - at[1]), at[1], at[0]),
    )
    near_row = [(dx, dc) for dx in range(n // 2) for dc in range(2)]

    def plane_at(d, sign=1):
        dy, dz = near[d]
        return lax.rem(gy + sign * dy + ny, ny) * nz + lax.rem(gz + sign * dz + nz, nz)

    def row_at(d, sign=1):
        dx, dc = near_row[d]
        return lax.rem(gx // 2 + sign * dx + n // 2, n // 2) * 2 + lax.rem(gx + sign * dc + 2, 2)

    def in_plane(d):
        other = plane_at(d)
        return (gx, other // nz, lax.rem(other, nz))

    def in_row(d):
        return (row_at(d), gy, gz)

    loads = []

    def load(src, dst):
        copy = pltpu.make_async_copy(src, dst, w_sem.at[len(loads)])
        loads.append(copy)
        copy.start()
        return copy

    def load_rows(src, dst, pieces):
        step = dst.shape[0] // pieces
        return [
            load(src.at[pl.ds(i * step, step), :], dst.at[pl.ds(i * step, step), :])
            for i in range(pieces)
        ]

    barrier = pltpu.get_barrier_semaphore()
    for d in range(1, planes):
        pl.semaphore_signal(barrier, inc=1, device_id=in_plane(d), device_id_type=MESH)
    for d in range(1, n):
        pl.semaphore_signal(barrier, inc=1, device_id=in_row(d), device_id_type=MESH)
    small = [
        pltpu.make_async_copy(src, dst, own_sem.at[i])
        for i, (src, dst) in enumerate(
            (
                (hidden, x_in.at[plane]),
                (seg_far, seg),
                (attn_gain_far, attn_gain),
                (ffn_gain_far, ffn_gain),
            )
        )
    ]
    for copy in small:
        copy.start()
    for copy in small:
        copy.wait()
    head_at = pl.ds(pl.multiple_of(gz * HS, HS), HS)
    first = [
        load(wk.at[:, head_at], kv_buf.at[:, pl.ds(0, HS)]),
        load(wv.at[:, head_at], kv_buf.at[:, pl.ds(HS, HS)]),
    ] + load_rows(wq, q_buf, 4)

    mine_f = x_in[plane].astype(F32)
    t_send[...] = fold(mine_f * mine_f)
    pl.semaphore_wait(barrier, planes + n - 2)

    def remote(src, dst, ss, rs, device):
        return pltpu.make_async_remote_copy(
            src_ref=src, dst_ref=dst, send_sem=ss, recv_sem=rs, device_id=device, device_id_type=MESH
        )

    sent = []

    def send(*what):
        copy = remote(*what)
        copy.start()
        sent.append(copy)

    order = list(range(1, planes))
    far = order[::-1]
    row = list(range(1, n))
    far_row = row[::-1]
    for d in far:
        send(x_in.at[plane], x_in.at[plane], x_ss.at[d], x_rs.at[d], in_plane(d))
    for d in far_row:
        send(t_send, t_recv.at[d], t_ss.at[d], t_rs.at[d], in_row(d))

    second = load_rows(wo, o_buf, 4)
    third = load_rows(wg.at[:, pl.ds(0, g_held)], g_buf, 4)
    across = jnp.broadcast_to(seg[...].astype(F32), (rows, rows))
    down_i = lax.broadcasted_iota(jnp.int32, (rows, rows), 0)
    across_i = lax.broadcasted_iota(jnp.int32, (rows, rows), 1)
    down = jnp.sum(jnp.where(down_i == across_i, across, 0.0), axis=1, keepdims=True)
    same = across == down
    places = jnp.sum(jnp.where(same & (down_i > across_i), 1.0, 0.0), axis=1, keepdims=True)
    bias = jnp.where(same & (across_i <= down_i), 0.0, -1e30)
    lane = lax.broadcasted_iota(jnp.int32, (rows, HS), 1)
    odd = lax.rem(lane, 2)
    freq = jnp.exp((lane - odd).astype(F32) * F32(-math.log(THETA) / HS))
    angle = places * freq
    cosine = jnp.cos(angle)
    sine = jnp.sin(angle)
    sine = jnp.where(odd == 0, -sine, sine)

    inv[...] = 1.0 / (ffn_gain[...] * ffn_gain[...])
    square = t_send[...]
    for d in row:
        remote(t_send, t_recv.at[d], t_ss.at[d], t_rs.at[d], in_row(d)).wait_recv()
        square = square + t_recv[d]
    t_all[plane] = jnp.broadcast_to(
        lax.rsqrt(jnp.sum(square, axis=1, keepdims=True) / width + EPS), square.shape
    )
    for d in far:
        send(t_all.at[plane], t_all.at[plane], u_ss.at[d], u_rs.at[d], in_plane(d))
    for d in order:
        source = plane_at(d, -1)
        remote(t_all.at[plane], t_all.at[source], u_ss.at[d], u_rs.at[d], in_plane(d)).wait_recv()
        remote(x_in.at[plane], x_in.at[source], x_ss.at[d], x_rs.at[d], in_plane(d)).wait_recv()
    local_rows = rows // planes
    for p in range(planes):
        tokens = x_in[p].astype(F32)
        x_f[p * local_rows : (p + 1) * local_rows, :] = tokens
        acc[p * local_rows : (p + 1) * local_rows, :] = tokens * t_all[p][:, :1]
    for at in range(0, depth, part):
        x_b[:, at : at + part] = (acc[:, at : at + part] * attn_gain[:, at : at + part]).astype(BF16)

    for copy in first:
        copy.wait()
    x_all = x_b[...]
    s_send[...] = jnp.dot(x_all, kv_buf[...], preferred_element_type=F32)
    for d in far_row:
        send(s_send, s_recv.at[d], s_ss.at[d], s_rs.at[d], in_row(d))
    for d in far_row + [0]:
        base = row_at(d) * part

        for t in range(part // tile):
            at = pl.multiple_of(base + t * tile, tile)
            to = t * tile
            q_send[d, :, pl.ds(to, tile)] = jnp.dot(
                x_b[...], q_buf[:, pl.ds(at, tile)], preferred_element_type=F32
            )

        if d:
            send(q_send.at[d], q_recv.at[d], q_ss.at[d], q_rs.at[d], in_row(d))
    fourth = load_rows(wg.at[:, pl.ds(g_held, q_cols)], q_buf, 4)

    shared = s_send[...]
    for d in range(1, n):
        remote(s_send, s_recv.at[d], s_ss.at[d], s_rs.at[d], in_row(d)).wait_recv()
        shared = shared + s_recv[d]

    def turn(values, cosine, sine):
        parity = lax.rem(lax.broadcasted_iota(jnp.int32, values.shape, 1), 2)
        partner = jnp.where(
            parity == 0, pltpu.roll(values, HS - 1, 1), pltpu.roll(values, 1, 1)
        )
        return (values * cosine + partner * sine).astype(BF16)

    keys = turn(shared[:, :HS], cosine, sine)
    values = shared[:, HS:].astype(BF16)
    heads = part // HS
    total = q_send[0]
    for d in range(1, n):
        remote(q_send.at[d], q_recv.at[d], q_ss.at[d], q_rs.at[d], in_row(d)).wait_recv()
        total = total + q_recv[d]
    stacked = jnp.concatenate([total[:, h * HS : (h + 1) * HS] for h in range(heads)], axis=0)
    queries = turn(
        stacked,
        jnp.concatenate([cosine] * heads, axis=0),
        jnp.concatenate([sine] * heads, axis=0),
    )
    scores = lax.dot_general(queries, keys, (((1,), (1,)), ((), ())), preferred_element_type=F32)
    scores = scores * F32(1.0 / math.sqrt(HS)) + jnp.concatenate([bias] * heads, axis=0)
    top = jnp.max(scores, axis=1, keepdims=True)
    expo = jnp.exp(scores - top)
    probs = (expo / jnp.sum(expo, axis=1, keepdims=True)).astype(BF16)
    mixed = jnp.dot(probs, values, preferred_element_type=F32).astype(BF16)
    mix[gx] = jnp.concatenate([mixed[h * rows : (h + 1) * rows] for h in range(heads)], axis=1)
    for d in far_row:
        send(mix.at[gx], mix.at[gx], m_ss.at[d], m_rs.at[d], in_row(d))
    for copy in second:
        copy.wait()

    def out_part(g, at, size):
        rows_at = pl.ds(pl.multiple_of(g * part, part), part)
        return jnp.dot(mix[g], o_buf[rows_at, pl.ds(at, size)], preferred_element_type=F32)

    def mixed_from(d):
        source = row_at(d, -1)
        remote(mix.at[gx], mix.at[source], m_ss.at[d], m_rs.at[d], in_row(d)).wait_recv()
        return source

    for t in range(depth // tile):
        at = t * tile
        acc[:, pl.ds(at, tile)] = out_part(gx, at, tile)

    near_by = mixed_from(1)

    for t in range(depth // tile):
        at = t * tile
        acc[:, pl.ds(at, tile)] += out_part(near_by, at, tile)

    rest = [mixed_from(d) for d in row[1:]]
    for h in range(halves):
        for d in far + [0]:
            at = pl.multiple_of(plane_at(d) * strip + h * piece, piece)
            got = acc[:, pl.ds(at, piece)]
            for g in rest:
                got = got + out_part(g, at, piece)
            o_send[h, d] = got.astype(BF16)
            if d:
                send(
                    o_send.at[h, d], o_recv.at[h, d], o_ss.at[h, d], o_rs.at[h, d], in_plane(d)
                )
    fifth = [
        load(
            wg.at[pl.ds(i * q_cols, q_cols), pl.ds(g_cols - g_last, g_last)],
            o_buf.at[:, pl.ds(i * g_last, g_last)],
        )
        for i in range(2)
    ]
    def settle(h):
        mine = pl.ds(pl.multiple_of(plane * strip + h * piece, piece), piece)
        resid = x_f[:, mine] + o_send[h, 0].astype(F32)
        for d in order:
            remote(
                o_send.at[h, d], o_recv.at[h, d], o_ss.at[h, d], o_rs.at[h, d], in_plane(d)
            ).wait_recv()
            resid = resid + o_recv[h, d].astype(F32)
        y_buf[h, plane] = (resid * ffn_gain[:, mine]).astype(BF16)
        for d in far:
            send(
                y_buf.at[h, plane], y_buf.at[h, plane], y_ss.at[h, d], y_rs.at[h, d], in_plane(d)
            )

    def gate_part(h, p, to):
        first_row = p * strip + h * piece
        if to < g_held:
            held, at = g_buf, to
        elif to < g_held + q_cols:
            held, at = q_buf, to - g_held
        else:
            half = planes // 2
            held, first_row = o_buf, lax.rem(p, half) * strip + h * piece
            at = pl.multiple_of(p // half * g_last + (to - g_held - q_cols), tile)
        rows_at = pl.ds(pl.multiple_of(first_row, piece), piece)
        return jnp.dot(y_buf[h, p], held[rows_at, pl.ds(at, tile)], preferred_element_type=F32)

    def squared(h, p):
        value = y_buf[h, p].astype(F32)
        at = pl.ds(pl.multiple_of(p * strip + h * piece, piece), piece)
        return fold(value * value * inv[:, at])

    def arrive(h, d):
        if d == 0:
            return h, plane
        source = plane_at(d, -1)
        remote(
            y_buf.at[h, plane], y_buf.at[h, source], y_ss.at[h, d], y_rs.at[h, d], in_plane(d)
        ).wait_recv()
        return h, source

    def gate_pass(sources, first):
        for to in range(0, g_cols, tile):
            got = gate_part(*sources[0], to)
            for at in sources[1:]:
                got = got + gate_part(*at, to)
            if not first:
                got = got + acc[:, pl.ds(to, tile)]
            acc[:, pl.ds(to, tile)] = got

    settle(0)
    for copy in third + fourth + fifth:
        copy.wait()
    gate_pass([(0, plane)], True)
    squares = squared(0, plane)
    for h in range(1, halves):
        settle(h)
        gate_pass([(h, plane)], False)
        squares = squares + squared(h, plane)
    units = [(h, d) for h in range(halves) for d in order]
    left = units[-6:]
    sizes = [2,2,2,2]
    while len(units) > 6:
        size = sizes.pop(0)
        sources = [arrive(*unit) for unit in units[:size]]
        units = units[size:]
        gate_pass(sources, False)
        for at in sources:
            squares = squares + squared(*at)

    sources = [arrive(*unit) for unit in left]
    for at in sources:
        squares = squares + squared(*at)
    for g in range(n):
        r_send[g] = squares[g * block : (g + 1) * block, :]
    for d in far_row:
        send(r_send.at[row_at(d)], r_recv.at[d], r_ss.at[d], r_rs.at[d], in_row(d))

    span = g_send.shape[3]
    for c in range(chunks):
        for to in range(0, span, tile):
            got = acc[:, pl.ds(c * span + to, tile)]
            for at in sources:
                got = got + gate_part(*at, c * span + to)
            for g in range(n):
                g_send[c, g, :, pl.ds(to, tile)] = got[g * block : (g + 1) * block].astype(BF16)

        for d in far_row:
            send(
                g_send.at[c, row_at(d)],
                g_recv.at[c, d],
                g_ss.at[c, d],
                g_rs.at[c, d],
                in_row(d),
            )
    square = r_send[gx]
    for d in range(1, n):
        remote(r_send.at[0], r_recv.at[d], r_ss.at[d], r_rs.at[d], in_row(d)).wait_recv()
        square = square + r_recv[d]
    scale = lax.rsqrt(jnp.sum(square, axis=1, keepdims=True) / width + EPS)
    for c in range(chunks):
        got = g_send[c, gx].astype(F32)
        for d in range(1, n):
            remote(
                g_send.at[c, 0], g_recv.at[c, d], g_ss.at[c, d], g_rs.at[c, d], in_row(d)
            ).wait_recv()
            got = got + g_recv[c, d].astype(F32)
        out[:, c * span : (c + 1) * span] = (got * scale).astype(BF16)
    for copy in sent:
        copy.wait_send()


def fused(
    sizes,
    hidden_in,
    segments,
    attn_gain,
    query_weight,
    key_weight,
    value_weight,
    output_weight,
    ffn_gain,
    gate_weight,
):
    n, ny, nz = sizes
    planes = ny * nz
    rows = segments.shape[0]
    local_rows, depth = hidden_in.shape
    q_cols = query_weight.shape[1]
    g_cols = gate_weight.shape[1]
    part = q_cols // n
    strip = depth // planes
    block = rows // n
    tile = 512
    chunks = 4
    halves = 2
    span = g_cols // chunks
    vmem = pltpu.VMEM
    dma = pltpu.SemaphoreType.DMA
    kernel = functools.partial(
        block_kernel, (n, ny, nz, float(depth * n), tile, chunks)
    )
    whole = pl.BlockSpec(memory_space=pltpu.VMEM)
    far = pl.BlockSpec(memory_space=pltpu.HBM)
    return pl.pallas_call(
        kernel,
        out_shape=pltpu.VMEM((block, g_cols), BF16),
        in_specs=[far] * 9,
        out_specs=whole,
        scratch_shapes=[
            vmem((1, rows), jnp.int32),
            vmem((1, depth), F32),
            vmem((1, depth), F32),
            vmem((depth, q_cols), BF16),
            vmem((depth, 2 * HS), BF16),
            vmem((q_cols, depth), BF16),
            vmem((depth, q_cols * 3 // 4), BF16),
            vmem((planes, local_rows, depth), BF16),
            vmem((rows, depth), F32),
            vmem((rows, depth), BF16),
            vmem((n, rows, part), F32),
            vmem((n, rows, part), F32),
            vmem((rows, 2 * HS), F32),
            vmem((n, rows, 2 * HS), F32),
            vmem((n, rows, part), BF16),
            vmem((halves, planes, rows, strip // halves), BF16),
            vmem((halves, planes, rows, strip // halves), BF16),
            vmem((halves, planes, rows, strip // halves), BF16),
            vmem((chunks, n, block, span), BF16),
            vmem((chunks, n, block, span), BF16),
            vmem((n, block, LANES), F32),
            vmem((n, block, LANES), F32),
            vmem((rows, depth), F32),
            vmem((1, depth), F32),
            vmem((local_rows, LANES), F32),
            vmem((n, local_rows, LANES), F32),
            vmem((planes, local_rows, LANES), F32),
            dma((20,)),
            dma((4,)),
            dma((planes,)),
            dma((planes,)),
            dma((n,)),
            dma((n,)),
            dma((n,)),
            dma((n,)),
            dma((n,)),
            dma((n,)),
            dma((halves, planes)),
            dma((halves, planes)),
            dma((halves, planes)),
            dma((halves, planes)),
            dma((chunks, n)),
            dma((chunks, n)),
            dma((n,)),
            dma((n,)),
            dma((n,)),
            dma((n,)),
            dma((planes,)),
            dma((planes,)),
        ],
        compiler_params=pltpu.CompilerParams(
            collective_id=0, has_side_effects=True, vmem_limit_bytes=52 * 1024 * 1024
        ),
    )(
        *(
            pltpu.with_memory_space_constraint(array, pltpu.HBM)
            for array in (
                hidden_in,
                segments.reshape(1, rows),
                attn_gain.reshape(1, depth),
                query_weight,
                key_weight,
                value_weight,
                output_weight,
                ffn_gain.reshape(1, depth),
                gate_weight,
            )
        )
    )


def local(sizes, *arrays):
    n, ny, nz = sizes
    planes = ny * nz
    hidden_in, segments, _, query_weight, key_weight, _, output_weight, _, gate_weight = arrays
    depth, q_cols = query_weight.shape
    fits = (
        q_cols // HS == QH // KVH
        and key_weight.shape[1] == nz * HS
        and gate_weight.shape[1] == 2 * q_cols
        and segments.shape[0] == 8 * n
        and n == 4
        and (q_cols // n) % 512 == 0
        and depth % (q_cols // n) == 0
        and (depth // planes) % 512 == 0
        and depth == 2 * q_cols
        and depth * q_cols * 6 <= 56 * 1024 * 1024
    )
    return fused(sizes, *arrays) if fits else shards(*arrays)


def solution(mesh):
    return jax.shard_map(
        functools.partial(local, tuple(mesh.shape[name] for name in ("gx", "gy", "gz"))),
        mesh=mesh,
        in_specs=(
            P(("gy", "gz"), "gx"),
            P(),
            P("gx"),
            P("gx", ("gy", "gz")),
            P("gx", "gy"),
            P("gx", "gy"),
            P(("gy", "gz"), "gx"),
            P("gx"),
            P("gx", ("gy", "gz")),
        ),
        out_specs=P("gx", ("gy", "gz")),
        check_vma=False,
    )
```
